32 devices in a mesh: tgt: 8 (over z, y), src: 4 (over x, core).
Axes of the slice: x: 2, y: 2, z: 4, core: 2. Of those that a mesh axis runs over, the one named last changes fastest.
Arguments:
- coefficients: bfloat16 [32, 4, 512, 512], P('tgt', 'src'), may hold values from -1.5 to 1.5
- factors: bfloat16 [3, 32, 4, 512, 512], P(None, 'tgt', 'src'), may hold values from -0.25 to 0.25
Outputs:
- potentials: float32 [32, 2, 256, 512], P('tgt', None, 'src')
The draws below stay inside these ranges and needn't reach their ends.
All inputs are finite; a program needn't handle non-finite values.
Results may differ from the reference program's by a relative error of at most 0.013.
Values may be sent and summed in bfloat16 or wider, within the bound.
A program may use at most 64 MiB of HBM per device.

```python
import jax
import jax.numpy as jnp
from jax import lax

R = 256
RHS = 512
BLK = 4
LEVELS = 3
TBLOCKS = 32
N_TGT = 8
N_SRC = 4


def levels(own_key, extent, cuts, low, top_value):
    level, own = 1.0, jax.random.fold_in(own_key, 6)
    for dim, blocks in cuts:
        steps = jnp.exp(jax.random.uniform(jax.random.fold_in(own, dim), (blocks,), jnp.float32, low / len(cuts), top_value / len(cuts)))
        level = level * jnp.repeat(steps, extent[dim] // blocks).reshape([-1 if axis == dim else 1 for axis in range(len(extent))])
    return level


def centred(key, extent, spread, reach, pieces=(), kind=jnp.bfloat16):
    loudness = levels(key, extent, pieces, -0.22, 0.18) if pieces else 1.0
    result = jax.random.normal(key, extent, jnp.float32) * spread * loudness
    return jnp.minimum(jnp.maximum(result, -reach), reach).astype(kind)


def setup_inputs(seed: int = 0) -> dict:
    splits = jax.random.split(jax.random.key(seed), 3)
    return {
        "coefficients": centred(splits[0], (TBLOCKS, N_SRC, 2 * R, RHS), 0.25, 1.5, ((0, 8), (1, 4))),
        "factors": centred(splits[1], (LEVELS, TBLOCKS, N_SRC, 2 * R, 2 * R), (2 * R) ** -0.5, 0.25, ((1, 8), (2, 4))),
    }


def reference(coefficients, factors):
    total_blocks = coefficients.shape[0]
    bit_count = N_TGT.bit_length() - 1
    current = coefficients
    for section_index in range(LEVELS):
        def mix_block(block_index):
            weights = factors[section_index, block_index].astype(jnp.float32)
            block = current[block_index].astype(jnp.float32)
            return jnp.einsum('sij,sjn->sin', weights, block).astype(jnp.bfloat16)

        blended = lax.map(mix_block, jnp.arange(total_blocks, dtype=jnp.int32))
        shift = section_index % bit_count
        partner = jnp.bitwise_xor(jnp.arange(total_blocks, dtype=jnp.int32), jnp.int32(BLK << shift))
        lower = jnp.take(blended[:, :, R:], partner, axis=0)
        current = jnp.concatenate([blended[:, :, :R], lower], axis=2)
    summed = jnp.sum(current.astype(jnp.float32), axis=1)
    return summed.reshape(total_blocks, 2, R, summed.shape[-1])
```

```python
import functools

import jax
import jax.numpy as jnp
from jax import lax
from jax.experimental import pallas as pl
from jax.experimental.pallas import tpu as pltpu
from jax.sharding import PartitionSpec as P

PARTS = 2
LAGS = (2, 4, 6)


def kernel(sizes, coef_ref, fact_ref, out_ref, *scratch):
    n_tgt, n_src, levels, blocks, half, width, parts, lags = sizes
    chunks, rows = blocks * parts, half // n_src
    fact, current, sends, part, inbox, low_send, low_recv, outbuf = scratch[:8]
    load_sem, coef_sem, lev_send, lev_recv, src_send, src_recv, low_sems, out_sem = scratch[8:]
    me = lax.axis_index("tgt")
    src = lax.axis_index("src")
    bits = n_tgt.bit_length() - 1

    def partner(level):
        step = 1 << level % bits
        return me + step * (1 - 2 * ((me // step) % 2))

    def peer(k):
        return (src + k) % n_src

    def load(level, block):
        return pltpu.make_async_copy(
            fact_ref.at[level, block], fact.at[level, block], load_sem.at[level, block]
        )

    def load_coef(c):
        return pltpu.make_async_copy(
            coef_ref.at[c // parts, :, pl.ds(pl.multiple_of((c % parts) * width, width), width)],
            current.at[0, c],
            coef_sem.at[c],
        )

    for b in range(blocks):
        load(0, b).start()
        for h in range(parts):
            load_coef(b * parts + h).start()
    for level in range(1, levels):
        for b in range(blocks):
            load(level, b).start()

    barrier = pltpu.get_barrier_semaphore()
    shifts = sorted({level % bits for level in range(levels)})
    for shift in shifts:
        pl.semaphore_signal(
            barrier, inc=1, device_id={"tgt": partner(shift)}, device_id_type=pl.DeviceIdType.MESH
        )
    for k in range(1, n_src):
        pl.semaphore_signal(
            barrier, inc=1, device_id={"src": peer(k)}, device_id_type=pl.DeviceIdType.MESH
        )

    def exchange(level, c):
        return pltpu.make_async_remote_copy(
            src_ref=sends.at[level, c],
            dst_ref=current.at[level + 1, c, pl.ds(half, half)],
            send_sem=lev_send.at[level, c],
            recv_sem=lev_recv.at[level, c],
            device_id={"tgt": partner(level)},
            device_id_type=pl.DeviceIdType.MESH,
        )

    def scatter(k, c):
        return pltpu.make_async_remote_copy(
            src_ref=part.at[c, peer(k)],
            dst_ref=inbox.at[c, k],
            send_sem=src_send.at[c, k],
            recv_sem=src_recv.at[c, k],
            device_id={"src": peer(k)},
            device_id_type=pl.DeviceIdType.MESH,
        )

    def lower(c):
        return pltpu.make_async_remote_copy(
            src_ref=low_send.at[c],
            dst_ref=low_recv.at[c],
            send_sem=low_sems.at[0, c],
            recv_sem=low_sems.at[1, c],
            device_id={"tgt": partner(levels - 1)},
            device_id_type=pl.DeviceIdType.MESH,
        )

    def write(side, c):
        columns = pl.ds(pl.multiple_of((c % parts) * width, width), width)
        return pltpu.make_async_copy(
            outbuf.at[side, c], out_ref.at[c // parts, side, :, columns], out_sem.at[side, c]
        )

    def level_stage(level, c):
        if level:
            exchange(level - 1, c).wait_recv()
        blended = jnp.dot(
            fact[level, c // parts], current[level, c], preferred_element_type=jnp.float32
        ).astype(jnp.bfloat16)
        if level < levels - 1:
            sends[level, c] = blended[half:]
            exchange(level, c).start()
            current[level + 1, c, :half] = blended[:half]
        else:
            for j in range(n_src):
                part[c, j, 0] = blended[j * rows : (j + 1) * rows]
                part[c, j, 1] = blended[half + j * rows : half + (j + 1) * rows]
            for k in range(1, n_src):
                scatter(k, c).start()

    def sum_stage(c):
        total = part[c, src].astype(jnp.float32)
        for k in range(1, n_src):
            scatter(k, c).wait_recv()
            total += inbox[c, k].astype(jnp.float32)
        low_send[c] = total[1].astype(jnp.bfloat16)
        lower(c).start()
        outbuf[0, c] = total[0]
        write(0, c).start()

    def last_stage(c):
        lower(c).wait_recv()
        outbuf[1, c] = low_recv[c].astype(jnp.float32)
        write(1, c).start()

    def first(c, carry):
        load_coef(c).wait()

        @pl.when(c % parts == 0)
        def _():
            load(0, c // parts).wait()

        level_stage(0, c)
        return carry

    pl.semaphore_wait(barrier, len(shifts) + n_src - 1)
    lax.fori_loop(0, chunks, first, 0)
    for level in range(1, levels):
        for b in range(blocks):
            load(level, b).wait()

    stages = [functools.partial(level_stage, level) for level in range(1, levels)]
    stages += [sum_stage, last_stage]

    def step(i, carry):
        for stage, lag in zip(stages, (0,) + lags):
            c = i - lag

            @pl.when(jnp.logical_and(c >= 0, c < chunks))
            def _():
                stage(c)

        return carry

    lax.fori_loop(0, chunks + lags[-1], step, 0)

    def finish(c, carry):
        for level in range(levels - 1):
            exchange(level, c).wait_send()
        for k in range(1, n_src):
            scatter(k, c).wait_send()
        lower(c).wait_send()
        write(0, c).wait()
        write(1, c).wait()
        return carry

    lax.fori_loop(0, chunks, finish, 0)


def local(n_tgt, n_src, coefficients, factors):
    levels, blocks = factors.shape[0], factors.shape[1]
    size, columns = coefficients.shape[2], coefficients.shape[3]
    half, width = size // 2, columns // PARTS
    chunks, rows = blocks * PARTS, half // n_src
    dma = pltpu.SemaphoreType.DMA
    bf16 = jnp.bfloat16
    return pl.pallas_call(
        functools.partial(
            kernel, (n_tgt, n_src, levels, blocks, half, width, PARTS, LAGS)
        ),
        out_shape=jax.ShapeDtypeStruct((blocks, 2, rows, columns), jnp.float32),
        in_specs=[pl.BlockSpec(memory_space=pl.ANY)] * 2,
        out_specs=pl.BlockSpec(memory_space=pl.ANY),
        scratch_shapes=[
            pltpu.VMEM((levels, blocks, size, size), bf16),
            pltpu.VMEM((levels, chunks, size, width), bf16),
            pltpu.VMEM((levels - 1, chunks, half, width), bf16),
            pltpu.VMEM((chunks, n_src, 2, rows, width), bf16),
            pltpu.VMEM((chunks, n_src, 2, rows, width), bf16),
            pltpu.VMEM((chunks, rows, width), bf16),
            pltpu.VMEM((chunks, rows, width), bf16),
            pltpu.VMEM((2, chunks, rows, width), jnp.float32),
            dma((levels, blocks)),
            dma((chunks,)),
            dma((levels - 1, chunks)),
            dma((levels - 1, chunks)),
            dma((chunks, n_src)),
            dma((chunks, n_src)),
            dma((2, chunks)),
            dma((2, chunks)),
        ],
        compiler_params=pltpu.CompilerParams(collective_id=0, has_side_effects=True),
    )(coefficients[:, 0], factors[:, :, 0])


def solution(mesh):
    placed = (P("tgt", "src", None, None), P(None, "tgt", "src", None, None))
    return jax.shard_map(
        functools.partial(local, mesh.shape["tgt"], mesh.shape["src"]),
        mesh=mesh,
        in_specs=placed,
        out_specs=P("tgt", None, "src", None),
        check_vma=False,
    )
```

```python
import functools

import jax
import jax.numpy as jnp
from jax import lax
from jax.experimental import pallas as pl
from jax.experimental.pallas import tpu as pltpu
from jax.sharding import PartitionSpec as P

PARTS = 4
LAGS = (3, 7, 10)
AHEAD = 6


def kernel(sizes, coef_ref, fact_ref, out_ref, *scratch):
    n_tgt, n_src, levels, blocks, half, width, parts, lags, ahead = sizes
    chunks, rows = blocks * parts, half // n_src
    fact, current, sends, part, inbox, low_send, low_recv = scratch[:7]
    load_sem, coef_sem, lev_send, lev_recv, src_send, src_recv, low_sems = scratch[7:]
    me = lax.axis_index("tgt")
    src = lax.axis_index("src")
    bits = n_tgt.bit_length() - 1

    def partner(level):
        step = 1 << level % bits
        return me + step * (1 - 2 * ((me // step) % 2))

    def peer(k):
        return (src + k) % n_src

    def load(level, block):
        return pltpu.make_async_copy(
            fact_ref.at[level, block], fact.at[level, block], load_sem.at[level, block]
        )

    def load_coef(c):
        return pltpu.make_async_copy(
            coef_ref.at[c // parts, :, pl.ds(pl.multiple_of((c % parts) * width, width), width)],
            current.at[0, c],
            coef_sem.at[c],
        )

    for b in range(blocks):
        load(0, b).start()
        for h in range(parts):
            load_coef(b * parts + h).start()
    for level in range(1, levels):
        for b in range(blocks):
            load(level, b).start()

    barrier = pltpu.get_barrier_semaphore()
    shifts = sorted({level % bits for level in range(levels)})
    for shift in shifts:
        pl.semaphore_signal(
            barrier, inc=1, device_id={"tgt": partner(shift)}, device_id_type=pl.DeviceIdType.MESH
        )
    for k in range(1, n_src):
        pl.semaphore_signal(
            barrier, inc=1, device_id={"src": peer(k)}, device_id_type=pl.DeviceIdType.MESH
        )

    def exchange(level, c):
        return pltpu.make_async_remote_copy(
            src_ref=sends.at[level, c],
            dst_ref=current.at[level + 1, c, pl.ds(half, half)],
            send_sem=lev_send.at[level, c],
            recv_sem=lev_recv.at[level, c],
            device_id={"tgt": partner(level)},
            device_id_type=pl.DeviceIdType.MESH,
        )

    def scatter(k, c):
        return pltpu.make_async_remote_copy(
            src_ref=part.at[c, peer(k)],
            dst_ref=inbox.at[c, k],
            send_sem=src_send.at[c, k],
            recv_sem=src_recv.at[c, k],
            device_id={"src": peer(k)},
            device_id_type=pl.DeviceIdType.MESH,
        )

    def lower(c):
        return pltpu.make_async_remote_copy(
            src_ref=low_send.at[c],
            dst_ref=low_recv.at[c],
            send_sem=low_sems.at[0, c],
            recv_sem=low_sems.at[1, c],
            device_id={"tgt": partner(levels - 1)},
            device_id_type=pl.DeviceIdType.MESH,
        )

    def write(side, c, value):
        columns = pl.ds(pl.multiple_of((c % parts) * width, width), width)
        out_ref[c // parts, side, :, columns] = value

    def level_stage(level, c, before_send=None):
        if level:
            exchange(level - 1, c).wait_recv()

        def blend(rows):
            return jnp.dot(
                fact[level, c // parts, rows], current[level, c], preferred_element_type=jnp.float32
            ).astype(jnp.bfloat16)

        if level < levels - 1:
            sends[level, c] = blend(pl.ds(half, half))
            if before_send is not None:
                before_send()
            exchange(level, c).start()
            current[level + 1, c, :half] = blend(pl.ds(0, half))
        else:
            blended = blend(pl.ds(0, 2 * half))
            for j in range(n_src):
                part[c, j, 0] = blended[j * rows : (j + 1) * rows]
                part[c, j, 1] = blended[half + j * rows : half + (j + 1) * rows]
            for k in range(1, n_src):
                scatter(k, c).start()

    def sum_stage(c):
        total = part[c, src].astype(jnp.float32)
        for k in range(1, n_src):
            scatter(k, c).wait_recv()
            total += inbox[c, k].astype(jnp.float32)
        low_send[c] = total[1].astype(jnp.bfloat16)
        lower(c).start()
        write(0, c, total[0])

    def last_stage(c):
        lower(c).wait_recv()
        write(1, c, low_recv[c].astype(jnp.float32))

    def first(c, before_send=None):
        load_coef(c).wait()

        @pl.when(c % parts == 0)
        def _():
            load(0, c // parts).wait()

        level_stage(0, c, before_send)

    def later(level, c):
        @pl.when(c % parts == 0)
        def _():
            load(level, c // parts).wait()

        level_stage(level, c)

    def looped(c, carry):
        first(c)
        return carry

    first(jnp.int32(0), lambda: pl.semaphore_wait(barrier, len(shifts) + n_src - 1))
    lax.fori_loop(1, ahead, looped, 0)

    stages = [functools.partial(later, level) for level in range(1, levels)]
    stages += [sum_stage, last_stage]
    if ahead < chunks:
        stages.append(first)

    def step(i, carry):
        for stage, lag in zip(stages, (0,) + lags + (-ahead,)):
            c = i - lag

            @pl.when(jnp.logical_and(c >= 0, c < chunks))
            def _():
                stage(c)

        return carry

    lax.fori_loop(0, chunks + lags[-1], step, 0)

    def finish(c, carry):
        for level in range(levels - 1):
            exchange(level, c).wait_send()
        for k in range(1, n_src):
            scatter(k, c).wait_send()
        lower(c).wait_send()
        return carry

    lax.fori_loop(0, chunks, finish, 0)


def local(n_tgt, n_src, coefficients, factors):
    levels, blocks = factors.shape[0], factors.shape[1]
    size, columns = coefficients.shape[2], coefficients.shape[3]
    half, width = size // 2, columns // PARTS
    chunks, rows = blocks * PARTS, half // n_src
    dma = pltpu.SemaphoreType.DMA
    bf16 = jnp.bfloat16
    return pl.pallas_call(
        functools.partial(
            kernel, (n_tgt, n_src, levels, blocks, half, width, PARTS, LAGS, min(AHEAD, chunks))
        ),
        out_shape=pltpu.VMEM((blocks, 2, rows, columns), jnp.float32),
        in_specs=[pl.BlockSpec(memory_space=pl.ANY)] * 2,
        out_specs=pl.BlockSpec(memory_space=pltpu.VMEM),
        scratch_shapes=[
            pltpu.VMEM((levels, blocks, size, size), bf16),
            pltpu.VMEM((levels, chunks, size, width), bf16),
            pltpu.VMEM((levels - 1, chunks, half, width), bf16),
            pltpu.VMEM((chunks, n_src, 2, rows, width), bf16),
            pltpu.VMEM((chunks, n_src, 2, rows, width), bf16),
            pltpu.VMEM((chunks, rows, width), bf16),
            pltpu.VMEM((chunks, rows, width), bf16),
            dma((levels, blocks)),
            dma((chunks,)),
            dma((levels - 1, chunks)),
            dma((levels - 1, chunks)),
            dma((chunks, n_src)),
            dma((chunks, n_src)),
            dma((2, chunks)),
        ],
        compiler_params=pltpu.CompilerParams(collective_id=0, has_side_effects=True),
    )(coefficients[:, 0], factors[:, :, 0])


def solution(mesh):
    placed = (P("tgt", "src", None, None), P(None, "tgt", "src", None, None))
    return jax.shard_map(
        functools.partial(local, mesh.shape["tgt"], mesh.shape["src"]),
        mesh=mesh,
        in_specs=placed,
        out_specs=P("tgt", None, "src", None),
        check_vma=False,
    )
```
